32 devices in a mesh: dp: 8 (over z, x), ctx: 4 (over y, core).
Axes of the slice: x: 2, y: 2, z: 4, core: 2. Of those that a mesh axis runs over, the one named last changes fastest.
Arguments:
- inputs: bfloat16 [8, 512, 2048], P('dp', 'ctx'), may hold values from -8 to 8
- doc_ids: int32 [8, 512], P('dp', 'ctx'), may hold values from 0 to 3, never falling along the last dimension, each value on 1 to 256 neighbouring positions
- dilation: int32 [1], replicated, may hold values from 1 to 256
- filter_w: bfloat16 [2, 2048, 2048], P(None, 'dp', 'ctx'), may hold values from -0.09375 to 0.09375
- gate_w: bfloat16 [2, 2048, 2048], P(None, 'dp', 'ctx'), may hold values from -0.09375 to 0.09375
- filter_m: float32 [2, 2048, 2048], P(None, 'dp', 'ctx'), may hold values from -0.01171875 to 0.01171875
- filter_v: float32 [2, 2048, 2048], P(None, 'dp', 'ctx'), may hold values from 1e-07 to 4e-06
- gate_m: float32 [2, 2048, 2048], P(None, 'dp', 'ctx'), may hold values from -0.01171875 to 0.01171875
- gate_v: float32 [2, 2048, 2048], P(None, 'dp', 'ctx'), may hold values from 1e-07 to 4e-06
- cotangent: bfloat16 [8, 512, 2048], P('dp', 'ctx'), may hold values from -6 to 6
Outputs:
- layer_out: bfloat16 [8, 512, 2048], P('dp', 'ctx')
- input_grad: bfloat16 [8, 512, 2048], P('dp', 'ctx')
- new_filter_w: bfloat16 [2, 2048, 2048], P(None, 'dp', 'ctx')
- new_gate_w: bfloat16 [2, 2048, 2048], P(None, 'dp', 'ctx')
- new_filter_m: float32 [2, 2048, 2048], P(None, 'dp', 'ctx')
- new_filter_v: float32 [2, 2048, 2048], P(None, 'dp', 'ctx')
- new_gate_m: float32 [2, 2048, 2048], P(None, 'dp', 'ctx')
- new_gate_v: float32 [2, 2048, 2048], P(None, 'dp', 'ctx')
The draws below stay inside these ranges and needn't reach their ends.
Inputs may be any that keep to these rules, and one draw needn't show every extreme that they name: `doc_ids`: document numbers never fall along a sequence; a document covers at most 256 positions.
All inputs are finite; a program needn't handle non-finite values.
Results may differ from the reference program's by a relative error of at most 0.0075.
Values may be sent and summed in bfloat16 or wider, within the bound.
No kernel may reach another device: no remote copies, remote signals or barrier semaphores. Data moves between devices by JAX's collectives and lax.ppermute only.
A program may use at most 128 MiB of HBM per device.

```python
import math
import jax
import jax.numpy as jnp
import numpy as np
from jax import lax

C = 2048
TD = 128
STEP = 10
LEN = 512
BATCH = 8
TOKENS = 4096


def raised(result, key, source, target, shards_of, factor):
    owner, partner = [(jnp.arange(result.shape[position]) // (result.shape[position] // shards_of)).reshape([-1 if axis == position else 1 for axis in range(result.ndim)]) for position in (source, target)]
    chosen = jax.random.permutation(key, shards_of)[partner]
    strong = (owner == chosen) | (owner == (partner + shards_of // 2) % shards_of)
    return jnp.where(strong, factor * result, result)


def levels(key, dims, shards, smallest, high):
    gain, own = 1.0, jax.random.fold_in(key, 6)
    for position, blocks in shards:
        steps = jnp.exp(jax.random.uniform(jax.random.fold_in(own, position), (blocks,), jnp.float32, smallest / len(shards), high / len(shards)))
        gain = gain * jnp.repeat(steps, dims[position] // blocks).reshape([-1 if axis == position else 1 for axis in range(len(dims))])
    return gain


def split_up(amount, total, bound, skew):
    loads = [(1 << 20) // math.isqrt(standing ** skew) + 1 for standing in range(2, amount + 1)]
    rest, given = total - bound - (amount - 1), [1] * (amount - 1)
    while rest > 0:
        free = [i for i in range(amount - 1) if given[i] < bound]
        mass, left = sum([loads[i] for i in free]), rest
        for i in free:
            extra = min(bound - given[i], max(1, left * loads[i] // mass), rest)
            given[i] = given[i] + extra
            rest = rest - extra
    return np.array([bound] + given)


def uneven(stream_key, number_of, total, limit, slope):
    if number_of == 2:
        one = jax.random.randint(stream_key, (), max(1, total - limit), min(limit, total - 1) + 1)
        return jnp.stack([one, total - one])
    tallies = jnp.asarray(split_up(number_of, total, limit, slope), jnp.int32)
    twos = (number_of - 1) // 2
    source_of, taker = tallies[1:1 + 2 * twos:2], tallies[2:2 + 2 * twos:2]
    margin = jnp.minimum(source_of - 1, limit - taker)
    moved = jax.random.randint(jax.random.fold_in(stream_key, 1), (twos,), 0, 1 << 20) % (margin + 1)
    tallies = tallies.at[1:1 + 2 * twos:2].set(source_of - moved).at[2:2 + 2 * twos:2].set(taker + moved)
    return tallies[jax.random.permutation(jax.random.fold_in(stream_key, 2), number_of)]


def bell_draw(rng, extent, width, most, split=(), held_as=jnp.bfloat16):
    result = jax.random.normal(rng, extent, jnp.float32) * width
    if len(split) > 0:
        result = levels(rng, extent, split, -0.22, 0.18) * result
    return jnp.clip(result, min=-most, max=most).astype(held_as)


def heavy_noise(stream_key, shape, deviation, limit, shards, heavy, held_as=jnp.bfloat16):
    result = deviation * jax.random.normal(stream_key, shape, jnp.float32)
    if shards:
        result = result * levels(stream_key, shape, shards, -0.22, 0.18)
    return jnp.clip(raised(result, jax.random.fold_in(stream_key, 3), *heavy), -limit, limit).astype(held_as)


def setup_inputs(seed: int = 0) -> dict:
    key_of = jax.random.split(jax.random.key(seed), 11)
    return {
        "inputs": heavy_noise(key_of[0], (BATCH, LEN, C), 1.0, 8.0, ((0, 8), (1, 4)), (0, 2, 8, 2.0)),
        "doc_ids": jax.vmap(lambda own: jnp.searchsorted(jnp.cumsum(uneven(own, 4, LEN, LEN // 2, 0)), jnp.arange(LEN), side="right"))(jax.random.split(key_of[1], BATCH)).reshape((BATCH, LEN)).astype(jnp.int32),
        "dilation": jax.random.randint(key_of[2], (1,), 1, 2 * TD + 1).astype(jnp.int32),
        "filter_w": bell_draw(key_of[3], (2, C, C), (2 * C) ** -0.5, 0.09375, ((1, 8), (2, 4))),
        "gate_w": bell_draw(key_of[4], (2, C, C), (2 * C) ** -0.5, 0.09375, ((1, 8), (2, 4))),
        "filter_m": bell_draw(key_of[5], (2, C, C), 0.002, 0.01171875, ((1, 8), (2, 4)), jnp.float32),
        "filter_v": jnp.clip(jnp.exp(math.log(3.999999989900971e-06) - 3.6888794 * jax.random.uniform(key_of[6], (2, C, C), jnp.float32) ** levels(key_of[6], (2, C, C), ((1, 8), (2, 4)), -0.2, 0.2)), 1.0000000116860974e-07, 3.999999989900971e-06),
        "gate_m": bell_draw(key_of[7], (2, C, C), 0.002, 0.01171875, ((1, 8), (2, 4)), jnp.float32),
        "gate_v": jnp.clip(jnp.exp(math.log(3.999999989900971e-06) - 3.6888794 * jax.random.uniform(key_of[8], (2, C, C), jnp.float32) ** levels(key_of[8], (2, C, C), ((1, 8), (2, 4)), -0.2, 0.2)), 1.0000000116860974e-07, 3.999999989900971e-06),
        "cotangent": bell_draw(key_of[9], (BATCH, LEN, C), 1.0, 6.0, ((0, 8), (1, 4))),
    }


BETA_ONE = 0.9
BETA_TWO = 0.95
LEARN_RATE = 0.001
EPSILON = 1e-08

def lagged_rows(sequence, seq_ids, shift_by):
    length = sequence.shape[0]
    start_row = (length - shift_by).astype(jnp.int32)
    padded = jnp.concatenate([jnp.zeros_like(sequence), sequence], axis=0)
    shifted = lax.dynamic_slice_in_dim(padded, start_row, length, 0)
    id_padded = jnp.concatenate([jnp.full((length,), -1, jnp.int32), seq_ids], axis=0)
    id_shifted = lax.dynamic_slice_in_dim(id_padded, start_row, length, 0)
    return jnp.where((id_shifted == seq_ids)[:, None], shifted, jnp.zeros_like(shifted))

def leading_rows(values, seq_ids, shift_by):
    length = values.shape[0]
    start_row = shift_by.astype(jnp.int32)
    padded = jnp.concatenate([values, jnp.zeros_like(values)], axis=0)
    rows_ahead = lax.dynamic_slice_in_dim(padded, start_row, length, 0)
    id_padded = jnp.concatenate([seq_ids, jnp.full((length,), -1, jnp.int32)], axis=0)
    ids_ahead = lax.dynamic_slice_in_dim(id_padded, start_row, length, 0)
    return jnp.where((ids_ahead == seq_ids)[:, None], rows_ahead, jnp.zeros_like(rows_ahead))

def adam_update(weight, moment, second, gradient):
    new_moment = BETA_ONE * moment + (1.0 - BETA_ONE) * gradient
    new_second = BETA_TWO * second + (1.0 - BETA_TWO) * gradient * gradient
    first_fix = 1.0 - BETA_ONE ** STEP
    second_fix = 1.0 - BETA_TWO ** STEP
    step_size = new_moment / first_fix / (jnp.sqrt(new_second / second_fix) + EPSILON)
    new_weight = (weight.astype(jnp.float32) - LEARN_RATE * step_size).astype(jnp.bfloat16)
    return (new_weight, new_moment, new_second)

def reference(inputs, doc_ids, dilation, filter_w, gate_w, filter_m, filter_v, gate_m, gate_v, cotangent):
    shift_by = dilation[0]
    tap_zero = jnp.concatenate([filter_w[0], gate_w[0]], axis=1)
    tap_one = jnp.concatenate([filter_w[1], gate_w[1]], axis=1)

    def one_sequence(totals, members):
        sequence, seq_ids, seq_cotangent = members
        lagged = lagged_rows(sequence, seq_ids, shift_by)
        pre_act = jnp.dot(sequence, tap_zero, preferred_element_type=jnp.float32) + jnp.dot(lagged, tap_one, preferred_element_type=jnp.float32)
        filter_tanh = jnp.tanh(pre_act[:, :C])
        gate_sigmoid = jax.nn.sigmoid(pre_act[:, C:])
        gated_vals = (filter_tanh * gate_sigmoid).astype(jnp.bfloat16)
        layer_rows = (sequence.astype(jnp.float32) + gated_vals.astype(jnp.float32)).astype(jnp.bfloat16)
        cot_float = seq_cotangent.astype(jnp.float32)
        filter_delta = (cot_float * gate_sigmoid * (1.0 - filter_tanh * filter_tanh)).astype(jnp.bfloat16)
        gate_delta = (cot_float * filter_tanh * gate_sigmoid * (1.0 - gate_sigmoid)).astype(jnp.bfloat16)
        pre_grad = jnp.concatenate([filter_delta, gate_delta], axis=1)
        back_near = lax.dot_general(pre_grad, tap_zero, (((1,), (1,)), ((), ())), preferred_element_type=jnp.float32)
        back_far = lax.dot_general(pre_grad, tap_one, (((1,), (1,)), ((), ())), preferred_element_type=jnp.float32)
        grad_rows = (cot_float + back_near + leading_rows(back_far, seq_ids, shift_by)).astype(jnp.bfloat16)
        grad_zero = totals[0] + lax.dot_general(sequence, pre_grad, (((0,), (0,)), ((), ())), preferred_element_type=jnp.float32)
        grad_one = totals[1] + lax.dot_general(lagged, pre_grad, (((0,), (0,)), ((), ())), preferred_element_type=jnp.float32)
        return ((grad_zero, grad_one), (layer_rows, grad_rows))
    start_totals = (jnp.zeros((C, 2 * C), jnp.float32), jnp.zeros((C, 2 * C), jnp.float32))
    (grad_zero, grad_one), (layer_out, input_grad) = lax.scan(one_sequence, start_totals, (inputs, doc_ids, cotangent))
    filter_grad = jnp.stack([grad_zero[:, :C], grad_one[:, :C]], axis=0) / TOKENS
    gate_grad = jnp.stack([grad_zero[:, C:], grad_one[:, C:]], axis=0) / TOKENS
    new_filter_w, new_filter_m, new_filter_v = adam_update(filter_w, filter_m, filter_v, filter_grad)
    new_gate_w, new_gate_m, new_gate_v = adam_update(gate_w, gate_m, gate_v, gate_grad)
    return (layer_out, input_grad, new_filter_w, new_gate_w, new_filter_m, new_filter_v, new_gate_m, new_gate_v)
```

```python
import jax
import jax.numpy as jnp
from jax import lax
from jax.sharding import PartitionSpec as P

STEP = 10

BETA_ONE = 0.9
BETA_TWO = 0.95
LEARN_RATE = 0.001
EPSILON = 1e-08

AXES = ("dp", "ctx")


def adam_update(weight, moment, second, gradient):
    new_moment = BETA_ONE * moment + (1.0 - BETA_ONE) * gradient
    new_second = BETA_TWO * second + (1.0 - BETA_TWO) * gradient * gradient
    first_fix = 1.0 - BETA_ONE**STEP
    second_fix = 1.0 - BETA_TWO**STEP
    step_size = new_moment / first_fix / (jnp.sqrt(new_second / second_fix) + EPSILON)
    new_weight = (weight.astype(jnp.float32) - LEARN_RATE * step_size).astype(jnp.bfloat16)
    return (new_weight, new_moment, new_second)


def lagged_rows(rows, seq_ids, shift_by):
    length = rows.shape[0]
    start_row = length - shift_by
    padded = jnp.concatenate([jnp.zeros_like(rows), rows], axis=0)
    shifted = lax.dynamic_slice_in_dim(padded, start_row, length, 0)
    id_padded = jnp.concatenate([jnp.full((length,), -1, jnp.int32), seq_ids], axis=0)
    id_shifted = lax.dynamic_slice_in_dim(id_padded, start_row, length, 0)
    return jnp.where((id_shifted == seq_ids)[:, None], shifted, jnp.zeros_like(shifted))


def leading_rows(values, seq_ids, shift_by):
    length = values.shape[0]
    padded = jnp.concatenate([values, jnp.zeros_like(values)], axis=0)
    ahead = lax.dynamic_slice_in_dim(padded, shift_by, length, 0)
    id_padded = jnp.concatenate([seq_ids, jnp.full((length,), -1, jnp.int32)], axis=0)
    id_ahead = lax.dynamic_slice_in_dim(id_padded, shift_by, length, 0)
    return jnp.where((id_ahead == seq_ids)[:, None], ahead, jnp.zeros_like(ahead))


def swapped(i, c):
    return (i & ~2) | ((c & 1) << 1), (c & ~1) | ((i >> 1) & 1)


def make_maps(dp, ctx):
    def line(label):
        return label[0] * ctx + label[1]

    labels = [(i, c) for i in range(dp) for c in range(ctx)]

    def enter(di, dc):
        return [(line(l), line(swapped(l[0] ^ di, l[1] ^ dc))) for l in labels]

    def inner(di, dc):
        return [(line(swapped(*l)), line(swapped(l[0] ^ di, l[1] ^ dc))) for l in labels]

    def leave(di, dc):
        return [(line(swapped(*l)), line((l[0] ^ di, l[1] ^ dc))) for l in labels]

    return enter, inner, leave


def send(value, pairs):
    return lax.ppermute(value, AXES, pairs)


def dot(a, b):
    return jnp.dot(a, b, preferred_element_type=jnp.float32)


def dot_t(a, b):
    return lax.dot_general(a, b, (((1,), (1,)), ((), ())), preferred_element_type=jnp.float32)


def t_dot(a, b):
    return lax.dot_general(a, b, (((0,), (0,)), ((), ())), preferred_element_type=jnp.float32)


def placed_rows(pieces, order, label):
    size = pieces[0].shape[0]
    whole = jnp.zeros((size * len(pieces),) + pieces[0].shape[1:], pieces[0].dtype)
    for m, piece in enumerate(pieces):
        whole = lax.dynamic_update_slice_in_dim(whole, piece, (label ^ order[m]) * size, 0)
    return whole


def placed_cols(pieces, label):
    size = pieces[0].shape[1]
    whole = jnp.zeros((pieces[0].shape[0], size * len(pieces)), pieces[0].dtype)
    for m, piece in enumerate(pieces):
        whole = lax.dynamic_update_slice_in_dim(whole, piece, (label ^ m) * size, 1)
    return whole


def per_device(
    inputs, doc_ids, dilation, filter_w, gate_w, filter_m, filter_v, gate_m, gate_v, cotangent
):
    dp, ctx = lax.axis_size("dp"), lax.axis_size("ctx")
    enter, inner, leave = make_maps(dp, ctx)
    i, c = lax.axis_index("dp"), lax.axis_index("ctx")
    vi, vc = swapped(i, c)
    rows = filter_w.shape[1]
    columns = filter_w.shape[2]
    tokens = inputs.shape[1]
    length = tokens * ctx
    shift_by = dilation[0]
    far = range(0, dp, 4)
    bf16 = jnp.bfloat16

    mine = inputs[0]
    near_pieces = [send(mine, enter(0, e)) for e in (0, 1)]
    near_ids = [send(doc_ids[0], enter(0, e)) for e in (0, 1)]
    pieces, id_pieces = list(near_pieces), list(near_ids)
    for dy in range(1, ctx // 2):
        pieces += [send(p, inner(0, 2 * dy)) for p in near_pieces]
        id_pieces += [send(p, inner(0, 2 * dy)) for p in near_ids]
    order = list(range(ctx))
    sequence = placed_rows(pieces, order, vc)
    seq_ids = placed_rows(id_pieces, order, vc)

    blocks = {}
    for j in far:
        for name, w in (("f", filter_w), ("g", gate_w)):
            got = send(w, enter(j, 0))
            across = send(got, inner(1, 0))
            blocks[name, j] = got
            blocks[name, j + 2] = send(got, inner(2, 0))
            blocks[name, j + 1] = across
            blocks[name, j + 3] = send(across, inner(2, 0))

    cot_pieces = [
        send(
            lax.dynamic_slice_in_dim(cotangent[0], (c ^ m) * columns, columns, 1),
            enter(0, m),
        )
        for m in range(ctx)
    ]
    cot_cols = placed_rows(cot_pieces, order, vc)

    lagged = lagged_rows(sequence, seq_ids, shift_by)

    def channels(whole, o):
        return lax.dynamic_slice_in_dim(whole, (vi ^ o) * rows, rows, 1)

    x_blocks = [channels(sequence, o) for o in range(dp)]
    l_blocks = [channels(lagged, o) for o in range(dp)]

    own_x = jnp.concatenate([x_blocks[j] for j in far], axis=1)
    core_x = send(jnp.concatenate([x_blocks[j + 2] for j in far], axis=1), inner(2, 0))
    side_x = send(jnp.concatenate([x_blocks[j + 1] for j in far], axis=1), inner(1, 0))
    diag_x = send(
        send(jnp.concatenate([x_blocks[j + 3] for j in far], axis=1), inner(1, 0)), inner(2, 0)
    )
    core_ids = send(seq_ids, inner(2, 0))
    side_ids = send(seq_ids, inner(1, 0))
    diag_ids = send(side_ids, inner(2, 0))
    group_x = [
        jnp.concatenate([x, lagged_rows(x, ids, shift_by)], axis=1)
        for x, ids in (
            (own_x, seq_ids),
            (core_x, core_ids),
            (side_x, side_ids),
            (diag_x, diag_ids),
        )
    ]

    pre = {}
    for name in ("f", "g"):
        total = None
        for j in far:
            for o in (j, j + 2, j + 1, j + 3):
                w = blocks[name, o]
                term = dot(
                    jnp.concatenate([x_blocks[o], l_blocks[o]], axis=1),
                    w.reshape(2 * rows, columns),
                )
                total = term if total is None else total + term
        pre[name] = total
    filter_tanh = jnp.tanh(pre["f"])
    gate_sigmoid = jax.nn.sigmoid(pre["g"])
    gated = (filter_tanh * gate_sigmoid).astype(bf16)
    cot_float = cot_cols.astype(jnp.float32)
    delta = {
        "f": (cot_float * gate_sigmoid * (1.0 - filter_tanh * filter_tanh)).astype(bf16),
        "g": (cot_float * filter_tanh * gate_sigmoid * (1.0 - gate_sigmoid)).astype(bf16),
    }

    grads = {}
    for name in ("f", "g"):
        own = delta[name]
        core = send(own, inner(2, 0))
        side = send(own, inner(1, 0))
        diag = send(side, inner(2, 0))
        total = None
        for x, d in zip(group_x, (own, core, side, diag)):
            term = t_dot(x, d)
            total = term if total is None else total + term
        parts = total.reshape(2, len(far), rows, columns)
        summed = None
        for n, j in reversed(list(enumerate(far))):
            got = send(parts[:, n].astype(bf16), leave(j, 0)).astype(jnp.float32)
            summed = got if summed is None else summed + got
        grads[name] = summed / (length * dp)

    out_pieces = [
        send(
            lax.dynamic_slice_in_dim(gated, (vc ^ m) * tokens, tokens, 0),
            leave(0, m),
        )
        for m in range(ctx)
    ]
    gated_rows = placed_cols(out_pieces, c)
    layer_out = (mine.astype(jnp.float32) + gated_rows.astype(jnp.float32)).astype(bf16)

    ahead = {name: leading_rows(delta[name], seq_ids, shift_by) for name in ("f", "g")}
    sums = []
    for o in range(dp):
        wf, wg = blocks["f", o], blocks["g", o]
        sums.append(
            dot_t(delta["f"], wf[0])
            + dot_t(delta["g"], wg[0])
            + dot_t(ahead["f"], wf[1])
            + dot_t(ahead["g"], wg[1])
        )
    back = jnp.concatenate(sums, axis=1).astype(bf16)
    vy = vc >> 1
    half = lax.dynamic_slice_in_dim(back, vy * 2 * tokens, 2 * tokens, 0).astype(jnp.float32)
    for dy in range(1, ctx // 2):
        piece = lax.dynamic_slice_in_dim(back, (vy ^ dy) * 2 * tokens, 2 * tokens, 0)
        half = half + send(piece, inner(0, 2 * dy)).astype(jnp.float32)
    half = half.astype(bf16)
    input_sum = None
    for e in (0, 1):
        piece = lax.dynamic_slice_in_dim(half, ((vc ^ e) & 1) * tokens, tokens, 0)
        got = send(piece, leave(0, e)).astype(jnp.float32)
        input_sum = got if input_sum is None else input_sum + got
    input_sum = jnp.concatenate(
        [lax.dynamic_slice_in_dim(input_sum, (i ^ t) * rows, rows, 1) for t in range(dp)], axis=1
    )
    input_grad = (cotangent[0].astype(jnp.float32) + input_sum).astype(bf16)

    new_filter_w, new_filter_m, new_filter_v = adam_update(
        filter_w, filter_m, filter_v, grads["f"]
    )
    new_gate_w, new_gate_m, new_gate_v = adam_update(gate_w, gate_m, gate_v, grads["g"])
    return (
        layer_out[None],
        input_grad[None],
        new_filter_w,
        new_gate_w,
        new_filter_m,
        new_filter_v,
        new_gate_m,
        new_gate_v,
    )


def solution(mesh):
    seq, par = P("dp", "ctx", None), P(None, "dp", "ctx")
    return jax.shard_map(
        per_device,
        mesh=mesh,
        in_specs=(seq, P("dp", "ctx"), P(), par, par, par, par, par, par, seq),
        out_specs=(seq, seq, par, par, par, par, par, par),
        check_vma=False,
    )
```

```python
import jax
import jax.numpy as jnp
from jax import lax
from jax.sharding import PartitionSpec as P

STEP = 10

BETA_ONE = 0.9
BETA_TWO = 0.95
LEARN_RATE = 0.001
EPSILON = 1e-08

AXES = ("dp", "ctx")


def adam_update(weight, moment, second, gradient):
    new_moment = BETA_ONE * moment + (1.0 - BETA_ONE) * gradient
    new_second = BETA_TWO * second + (1.0 - BETA_TWO) * gradient * gradient
    first_fix = 1.0 - BETA_ONE**STEP
    second_fix = 1.0 - BETA_TWO**STEP
    step_size = new_moment / first_fix / (jnp.sqrt(new_second / second_fix) + EPSILON)
    new_weight = (weight.astype(jnp.float32) - LEARN_RATE * step_size).astype(jnp.bfloat16)
    return (new_weight, new_moment, new_second)


def lagged_rows(rows, marks, shift_by):
    length = rows.shape[0]
    padded = jnp.concatenate([jnp.zeros_like(rows), rows], axis=0)
    shifted = lax.dynamic_slice_in_dim(padded, length - shift_by, length, 0)
    mark_padded = jnp.concatenate([jnp.zeros_like(marks), marks], axis=0)
    mark_shifted = lax.dynamic_slice_in_dim(mark_padded, length - shift_by, length, 0)
    return jnp.where(mark_shifted == marks, shifted, jnp.zeros_like(shifted))


def leading_rows(values, marks, shift_by):
    length = values.shape[0]
    padded = jnp.concatenate([values, jnp.zeros_like(values)], axis=0)
    ahead = lax.dynamic_slice_in_dim(padded, shift_by, length, 0)
    mark_padded = jnp.concatenate([marks, jnp.zeros_like(marks)], axis=0)
    mark_ahead = lax.dynamic_slice_in_dim(mark_padded, shift_by, length, 0)
    return jnp.where(mark_ahead == marks, ahead, jnp.zeros_like(ahead))


def activate(own, got, cot):
    wide = cot.shape[1]
    pre = own + got
    filter_tanh = jnp.tanh(pre[:, :wide])
    gate_sigmoid = jax.nn.sigmoid(pre[:, wide:])
    cot = cot.astype(jnp.float32)
    gated = (filter_tanh * gate_sigmoid).astype(jnp.bfloat16)
    filter_delta = cot * gate_sigmoid * (1.0 - filter_tanh * filter_tanh)
    gate_delta = cot * filter_tanh * gate_sigmoid * (1.0 - gate_sigmoid)
    delta = jnp.concatenate([filter_delta, gate_delta], axis=1).astype(jnp.bfloat16)
    return gated, delta


def swapped(i, c):
    return (i & ~2) | ((c & 1) << 1), (c & ~1) | ((i >> 1) & 1)


def make_maps(dp, ctx):
    def line(label):
        return label[0] * ctx + label[1]

    labels = [(i, c) for i in range(dp) for c in range(ctx)]

    def enter(di, dc):
        return [(line(l), line(swapped(l[0] ^ di, l[1] ^ dc))) for l in labels]

    def inner(di, dc):
        return [(line(swapped(*l)), line(swapped(l[0] ^ di, l[1] ^ dc))) for l in labels]

    def leave(di, dc):
        return [(line(swapped(*l)), line((l[0] ^ di, l[1] ^ dc))) for l in labels]

    def plain(di, dc):
        return [(line(l), line((l[0] ^ di, l[1] ^ dc))) for l in labels]

    return enter, inner, leave, plain


def send(value, pairs):
    return lax.ppermute(value, AXES, [(a, b) for a, b in pairs if a != b])


def dot(a, b):
    return jnp.dot(a, b, preferred_element_type=jnp.float32)


def dot_t(a, b):
    return lax.dot_general(a, b, (((1,), (1,)), ((), ())), preferred_element_type=jnp.float32)


def t_dot(a, b):
    return lax.dot_general(a, b, (((0,), (0,)), ((), ())), preferred_element_type=jnp.float32)


def placed_rows(pieces, label):
    size = pieces[0].shape[0]
    whole = jnp.zeros((size * len(pieces),) + pieces[0].shape[1:], pieces[0].dtype)
    for m, piece in enumerate(pieces):
        whole = lax.dynamic_update_slice_in_dim(whole, piece, (label ^ m) * size, 0)
    return whole


def placed_cols(pieces, label):
    stacked = jnp.stack(pieces)
    return jnp.concatenate(
        [
            lax.dynamic_index_in_dim(stacked, label ^ t, 0, keepdims=False)
            for t in range(len(pieces))
        ],
        axis=1,
    )


CHUNKS = 2


def per_device(
    inputs, doc_ids, dilation, filter_w, gate_w, filter_m, filter_v, gate_m, gate_v, cotangent
):
    dp, ctx = lax.axis_size("dp"), lax.axis_size("ctx")
    enter, inner, leave, plain = make_maps(dp, ctx)
    i, c = lax.axis_index("dp"), lax.axis_index("ctx")
    vi, vc = swapped(i, c)
    core = c & 1
    vy = c >> 1
    home = core == ((i >> 1) & 1)
    rows = filter_w.shape[1]
    columns = filter_w.shape[2]
    wide = columns // CHUNKS
    tokens = inputs.shape[1]
    length = tokens * ctx
    shift_by = dilation[0]
    far = list(range(0, dp, 4))
    spans = [j + xx for j in far for xx in (0, 1)]
    others = range(1, ctx // 2)
    bf16, f32 = jnp.bfloat16, jnp.float32

    packed = [
        jnp.concatenate(
            [w[:, :, n * wide : (n + 1) * wide] for w in (filter_w, gate_w)], axis=2
        )
        for n in range(CHUNKS)
    ]
    block = {}

    def kept(own, got):
        return jnp.where(home, own, got)

    def fetch(n, j):
        got = send(packed[n], enter(j, 0))
        block[n, j] = got if j else kept(packed[n], got)

    def relay(n, j):
        block[n, j + 1] = send(block[n, j], inner(1, 0))

    mine = inputs[0]

    def channels(label):
        return jnp.concatenate(
            [lax.dynamic_slice_in_dim(mine, (label ^ o) * rows, rows, 1) for o in spans] + [marks],
            axis=1,
        )

    def pair(own, got):
        low, high = jnp.where(core == 0, own, got), jnp.where(core == 0, got, own)
        return jnp.concatenate([low, high], axis=0)

    for j in far[1:]:
        fetch(0, j)
    fetch(0, 0)
    lanes = 128
    marks = jnp.broadcast_to((doc_ids[0] + 1).astype(bf16)[:, None], (tokens, lanes))
    half = pair(channels(vi), send(channels(vi ^ 2), plain(0, 1)))

    def odd(value):
        return jnp.concatenate(
            [value[:, (2 * n + 1) * rows : (2 * n + 2) * rows] for n in range(len(far))]
            + [value[:, len(spans) * rows :]],
            axis=1,
        )

    def even(value):
        return jnp.concatenate(
            [value[:, 2 * n * rows : (2 * n + 1) * rows] for n in range(len(far))], axis=1
        )

    z_half = send(half, plain(2, 0))
    y_half = [send(half, plain(0, 2 * dy)) for dy in others]
    side_half = send(odd(half), plain(1, 0))
    yz_half = [send(z_half, plain(0, 2 * dy)) for dy in others]
    side_both = jnp.concatenate([side_half, send(odd(z_half), plain(1, 0))], axis=1)
    side_parts = [side_both] + [send(side_both, plain(0, 2 * dy)) for dy in others]
    for j in far[1:]:
        fetch(1, j)
    fetch(1, 0)
    for n in range(CHUNKS):
        for j in far:
            relay(n, j)

    def in_order(here, there):
        return [jnp.where(home, here, there), jnp.where(home, there, here)]

    sequences = in_order(
        placed_rows([half] + y_half, vy), placed_rows([z_half] + yz_half, vy)
    )
    ids_here = [x[:, len(spans) * rows :][:, :1] for x in sequences]
    sequences = [x[:, : len(spans) * rows] for x in sequences]
    side_whole = placed_rows(side_parts, vy)
    width = side_whole.shape[1] // 2
    side = in_order(side_whole[:, :width], side_whole[:, width:])
    ids_side = [x[:, len(far) * rows :][:, :1] for x in side]
    side = [x[:, : len(far) * rows] for x in side]
    lagged = [lagged_rows(x, d, shift_by) for x, d in zip(sequences, ids_here)]
    taps = [[], []]
    for q in (0, 1):
        for n in range(len(spans)):
            cut = slice(n * rows, (n + 1) * rows)
            taps[q].append(jnp.concatenate([sequences[q][:, cut], lagged[q][:, cut]], axis=1))
    group = [
        jnp.concatenate([even(x), even(l)], axis=1) for x, l in zip(sequences, lagged)
    ] + [
        jnp.concatenate([x, lagged_rows(x, ids_side[q], shift_by)], axis=1)
        for q, x in enumerate(side)
    ]

    own_cols = 2 * columns
    cot_parts = [lax.dynamic_slice_in_dim(cotangent[0], vy * own_cols, own_cols, 1)] + [
        send(
            lax.dynamic_slice_in_dim(cotangent[0], (vy ^ dy) * own_cols, own_cols, 1),
            plain(0, 2 * dy),
        )
        for dy in others
    ]
    cot_rows = jnp.stack(cot_parts)
    cot_cuts = [
        lax.dynamic_slice_in_dim(cot_rows, (core ^ e) * columns, columns, 2) for e in (0, 1)
    ]
    cot_got = [send(cot_cuts[e], enter(0, e)) for e in (0, 1)]
    cot_got[0] = kept(cot_cuts[0], cot_got[0])
    cot_cols = placed_rows(
        [cot_got[m & 1][m >> 1] for m in range(ctx)], vc
    )

    gated, delta, grads, backs = [], [], [], []
    for n in range(CHUNKS):
        pre = []
        for q in (1, 0):
            total = None
            for j in far:
                for xx in (0, 1):
                    w = block[n, j + xx].reshape(2 * rows, 2 * wide)
                    term = dot(taps[q][spans.index(j + xx)], w)
                    total = term if total is None else total + term
            pre.append(total)
        got = send(pre[0], inner(2, 0))
        cot = cot_cols[:, n * wide : (n + 1) * wide]
        if n:
            cot, _ = lax.optimization_barrier((cot, delta[-1][0]))
        gated_n, here = activate(pre[1], got, cot)
        gated.append(gated_n)
        across = send(here, inner(1, 0))
        beside = send(here, inner(2, 0))
        diagonal = send(across, inner(2, 0))
        delta.append([here, beside])
        part = []
        for q, d in enumerate(delta[n]):
            if n:
                d, _ = lax.optimization_barrier((d, backs[-1][q][0]))
            ahead = leading_rows(d, ids_here[q], shift_by)
            part.append(
                {
                    o: dot_t(d, block[n, o][0]) + dot_t(ahead, block[n, o][1])
                    for o in spans
                }
            )
        backs.append(part)
        total = None
        for x, d in zip(group, (here, beside, across, diagonal)):
            term = t_dot(x, d)
            total = term if total is None else total + term
        parts = total.astype(bf16).reshape(2, len(far), rows, 2 * wide)
        got = [send(parts[:, m], leave(j, 0)) for m, j in enumerate(far)]
        got[0] = kept(parts[:, 0], got[0])
        grads.append(got)

    gated = jnp.concatenate(gated, axis=1)
    out_cuts = [
        lax.dynamic_slice_in_dim(gated, (vc ^ m) * tokens, tokens, 0) for m in range(ctx)
    ]
    out_pieces = [send(out_cuts[m], leave(0, m)) for m in range(ctx)]
    out_pieces[0] = kept(out_cuts[0], out_pieces[0])
    gated_rows = placed_cols(out_pieces, c)
    layer_out = (mine.astype(f32) + gated_rows.astype(f32)).astype(bf16)

    def half_of(value, label):
        return lax.dynamic_slice_in_dim(value, label * 2 * tokens, 2 * tokens, 0)

    chip_sums = []
    for q in (0, 1):
        back = jnp.concatenate(
            [sum(backs[n][q][o] for n in range(CHUNKS)) for o in spans], axis=1
        )
        kept_rows = half_of(back, vy)
        for dy in others:
            piece = half_of(back, vy ^ dy).astype(bf16)
            kept_rows = kept_rows + send(piece, plain(0, 2 * dy)).astype(f32)
        chip_sums.append(kept_rows)
    chip_sum = in_order(*chip_sums)
    crossing = chip_sum[1].astype(bf16)
    z_got = send(crossing, plain(2, 0)).astype(f32)
    both_sum = (chip_sum[0] + z_got).astype(bf16)
    keep = lax.dynamic_slice_in_dim(both_sum, core * tokens, tokens, 0)
    give = lax.dynamic_slice_in_dim(both_sum, (1 - core) * tokens, tokens, 0)
    got = send(give, plain(0, 1))
    joined = jnp.concatenate([keep, got], axis=1)
    where_is = []
    for t in range(dp):
        rel = vi ^ t
        slot = (rel >> 2) * 2 + (rel & 1) + ((rel >> 1) & 1) * len(spans)
        where_is.append(lax.dynamic_slice_in_dim(joined, slot * rows, rows, 1))
    input_sum = jnp.concatenate(where_is, axis=1).astype(f32)
    input_grad = (cotangent[0].astype(f32) + input_sum).astype(bf16)

    totals = []
    for parts in grads:
        summed = parts[0].astype(f32)
        for part in parts[1:]:
            summed = summed + part.astype(f32)
        totals.append(summed / (length * dp))
    filter_grad = jnp.concatenate([t[:, :, :wide] for t in totals], axis=2)
    gate_grad = jnp.concatenate([t[:, :, wide:] for t in totals], axis=2)
    new_filter_w, new_filter_m, new_filter_v = adam_update(
        filter_w, filter_m, filter_v, filter_grad
    )
    new_gate_w, new_gate_m, new_gate_v = adam_update(gate_w, gate_m, gate_v, gate_grad)
    return (
        layer_out[None],
        input_grad[None],
        new_filter_w,
        new_gate_w,
        new_filter_m,
        new_filter_v,
        new_gate_m,
        new_gate_v,
    )


def solution(mesh):
    seq, par = P("dp", "ctx", None), P(None, "dp", "ctx")

    return jax.shard_map(
        per_device,
        mesh=mesh,
        in_specs=(seq, P("dp", "ctx"), P(), par, par, par, par, par, par, seq),
        out_specs=(seq, seq, par, par, par, par, par, par),
        check_vma=False,
    )
```

```python
import jax
import jax.numpy as jnp
from jax import lax
from jax.experimental.layout import Layout, with_layout_constraint
from jax.sharding import PartitionSpec as P

STEP = 10

BETA_ONE = 0.9
BETA_TWO = 0.95
LEARN_RATE = 0.001
EPSILON = 1e-08

AXES = ("dp", "ctx")


def adam_update(weight, moment, second, gradient):
    new_moment = BETA_ONE * moment + (1.0 - BETA_ONE) * gradient
    new_second = BETA_TWO * second + (1.0 - BETA_TWO) * gradient * gradient
    first_fix = 1.0 - BETA_ONE**STEP
    second_fix = 1.0 - BETA_TWO**STEP
    step_size = new_moment / first_fix / (jnp.sqrt(new_second / second_fix) + EPSILON)
    new_weight = (weight.astype(jnp.float32) - LEARN_RATE * step_size).astype(jnp.bfloat16)
    return (new_weight, new_moment, new_second)


def lagged_rows(rows, marks, shift_by):
    length = rows.shape[0]
    padded = jnp.concatenate([jnp.zeros_like(rows), rows], axis=0)
    shifted = lax.dynamic_slice_in_dim(padded, length - shift_by, length, 0)
    mark_padded = jnp.concatenate([jnp.zeros_like(marks), marks], axis=0)
    mark_shifted = lax.dynamic_slice_in_dim(mark_padded, length - shift_by, length, 0)
    return jnp.where(mark_shifted == marks, shifted, jnp.zeros_like(shifted))


def leading_rows(values, marks, shift_by):
    length = values.shape[0]
    padded = jnp.concatenate([values, jnp.zeros_like(values)], axis=0)
    ahead = lax.dynamic_slice_in_dim(padded, shift_by, length, 0)
    mark_padded = jnp.concatenate([marks, jnp.zeros_like(marks)], axis=0)
    mark_ahead = lax.dynamic_slice_in_dim(mark_padded, shift_by, length, 0)
    return jnp.where(mark_ahead == marks, ahead, jnp.zeros_like(ahead))


def activate(own, got, cot):
    wide = cot.shape[1]
    pre = own + got
    filter_tanh = jnp.tanh(pre[:, :wide])
    gate_sigmoid = jax.nn.sigmoid(pre[:, wide:])
    cot = cot.astype(jnp.float32)
    gated = (filter_tanh * gate_sigmoid).astype(jnp.bfloat16)
    filter_delta = cot * gate_sigmoid * (1.0 - filter_tanh * filter_tanh)
    gate_delta = cot * filter_tanh * gate_sigmoid * (1.0 - gate_sigmoid)
    delta = jnp.concatenate([filter_delta, gate_delta], axis=1).astype(jnp.bfloat16)
    return gated, delta


def swapped(i, c):
    return (i & ~2) | ((c & 1) << 1), (c & ~1) | ((i >> 1) & 1)


def make_maps(dp, ctx):
    def line(label):
        return label[0] * ctx + label[1]

    labels = [(i, c) for i in range(dp) for c in range(ctx)]

    def enter(di, dc):
        return [(line(l), line(swapped(l[0] ^ di, l[1] ^ dc))) for l in labels]

    def inner(di, dc):
        return [(line(swapped(*l)), line(swapped(l[0] ^ di, l[1] ^ dc))) for l in labels]

    def leave(di, dc):
        return [(line(swapped(*l)), line((l[0] ^ di, l[1] ^ dc))) for l in labels]

    def plain(di, dc):
        return [(line(l), line((l[0] ^ di, l[1] ^ dc))) for l in labels]

    return enter, inner, leave, plain


def send(value, pairs):
    return lax.ppermute(value, AXES, [(a, b) for a, b in pairs if a != b])


def dot(a, b):
    return jnp.dot(a, b, preferred_element_type=jnp.float32)


def dot_t(a, b):
    return lax.dot_general(a, b, (((1,), (1,)), ((), ())), preferred_element_type=jnp.float32)


def t_dot(a, b):
    return lax.dot_general(a, b, (((0,), (0,)), ((), ())), preferred_element_type=jnp.float32)


def flipped(parts, label):
    bit = 1
    while bit < len(parts):
        flip = (label & bit) != 0
        parts = [jnp.where(flip, parts[n ^ bit], parts[n]) for n in range(len(parts))]
        bit *= 2
    return parts


def placed_rows(pieces, label):
    return jnp.concatenate(flipped(pieces, label), axis=0)


def placed_cols(pieces, label):
    return jnp.concatenate(flipped(pieces, label), axis=1)


def arrange(x, marks, label, spans, rows):
    count = x.shape[1] // rows
    parts = flipped([x[:, n * rows : (n + 1) * rows] for n in range(count)], label)
    return [
        jnp.concatenate([parts[o ^ at] for o in spans] + [marks], axis=1) for at in (0, 2)
    ]


CHUNKS = 2


def per_device(
    inputs, doc_ids, dilation, filter_w, gate_w, filter_m, filter_v, gate_m, gate_v, cotangent
):
    dp, ctx = lax.axis_size("dp"), lax.axis_size("ctx")
    enter, inner, leave, plain = make_maps(dp, ctx)
    i, c = lax.axis_index("dp"), lax.axis_index("ctx")
    vi, vc = swapped(i, c)
    core = c & 1
    vy = c >> 1
    home = core == ((i >> 1) & 1)
    rows = filter_w.shape[1]
    columns = filter_w.shape[2]
    wide = columns // CHUNKS
    tokens = inputs.shape[1]
    length = tokens * ctx
    shift_by = dilation[0]
    far = list(range(0, dp, 4))
    spans = [j + xx for j in far for xx in (0, 1)]
    others = range(1, ctx // 2)
    bf16, f32 = jnp.bfloat16, jnp.float32

    row_major = Layout(major_to_minor=(0, 1, 2))
    packed = [
        with_layout_constraint(
            jnp.concatenate(
                [w[:, :, n * wide : (n + 1) * wide] for w in (filter_w, gate_w)], axis=2
            ),
            row_major,
        )
        for n in range(CHUNKS)
    ]
    block = {}

    def kept(own, got):
        return jnp.where(home, own, got)

    def fetch(n, j):
        got = send(packed[n], enter(j, 0))
        block[n, j] = got if j else kept(packed[n], got)

    def relay(n, j):
        block[n, j + 1] = send(block[n, j], inner(1, 0))

    mine = inputs[0]

    def pair(own, got):
        low, high = jnp.where(core == 0, own, got), jnp.where(core == 0, got, own)
        return jnp.concatenate([low, high], axis=0)

    for j in far[1:]:
        fetch(0, j)
    fetch(0, 0)
    lanes = 128
    marks = jnp.broadcast_to((doc_ids[0] + 1).astype(bf16)[:, None], (tokens, lanes))
    own_x, give_x = arrange(mine, marks, vi, spans, rows)
    half = pair(own_x, send(give_x, plain(0, 1)))

    def odd(value):
        return jnp.concatenate(
            [value[:, (2 * n + 1) * rows : (2 * n + 2) * rows] for n in range(len(far))]
            + [value[:, len(spans) * rows :]],
            axis=1,
        )

    def even(value):
        return jnp.concatenate(
            [value[:, 2 * n * rows : (2 * n + 1) * rows] for n in range(len(far))], axis=1
        )

    z_half = send(half, plain(2, 0))
    y_half = [send(half, plain(0, 2 * dy)) for dy in others]
    side_half = send(odd(half), plain(1, 0))
    yz_half = [send(z_half, plain(0, 2 * dy)) for dy in others]
    side_both = jnp.concatenate([side_half, send(odd(z_half), plain(1, 0))], axis=1)
    side_parts = [side_both] + [send(side_both, plain(0, 2 * dy)) for dy in others]
    for j in far[1:]:
        fetch(1, j)
    fetch(1, 0)
    for n in range(CHUNKS):
        for j in far:
            relay(n, j)

    def in_order(here, there):
        return [jnp.where(home, here, there), jnp.where(home, there, here)]

    sequences = in_order(
        placed_rows([half] + y_half, vy), placed_rows([z_half] + yz_half, vy)
    )
    ids_here = [x[:, len(spans) * rows :][:, :1] for x in sequences]
    sequences = [x[:, : len(spans) * rows] for x in sequences]
    side_whole = placed_rows(side_parts, vy)
    width = side_whole.shape[1] // 2
    side = in_order(side_whole[:, :width], side_whole[:, width:])
    ids_side = [x[:, len(far) * rows :][:, :1] for x in side]
    side = [x[:, : len(far) * rows] for x in side]
    lagged = [lagged_rows(x, d, shift_by) for x, d in zip(sequences, ids_here)]
    taps = [[], []]
    for q in (0, 1):
        for n in range(len(spans)):
            cut = slice(n * rows, (n + 1) * rows)
            taps[q].append(jnp.concatenate([sequences[q][:, cut], lagged[q][:, cut]], axis=1))
    group = [
        jnp.concatenate([even(x), even(l)], axis=1) for x, l in zip(sequences, lagged)
    ] + [
        jnp.concatenate([x, lagged_rows(x, ids_side[q], shift_by)], axis=1)
        for q, x in enumerate(side)
    ]

    cot_cuts = flipped(
        [cotangent[0][:, m * columns : (m + 1) * columns] for m in range(ctx)], c
    )
    cot_got = [send(cot_cuts[m], enter(0, m)) for m in range(ctx)]
    cot_got[0] = kept(cot_cuts[0], cot_got[0])
    cot_cols = placed_rows(cot_got, vc)

    gated, delta, grads, backs = [], [], [], []
    for n in range(CHUNKS):
        pre = []
        for q in (1, 0):
            total = None
            for j in far:
                for xx in (0, 1):
                    w = block[n, j + xx].reshape(2 * rows, 2 * wide)
                    term = dot(taps[q][spans.index(j + xx)], w)
                    total = term if total is None else total + term
            pre.append(total)
        got = send(pre[0], inner(2, 0))
        cot = cot_cols[:, n * wide : (n + 1) * wide]
        if n:
            cot, _ = lax.optimization_barrier((cot, delta[-1][0]))
        gated_n, here = activate(pre[1], got, cot)
        gated.append(gated_n)
        across = send(here, inner(1, 0))
        beside = send(here, inner(2, 0))
        diagonal = send(across, inner(2, 0))
        delta.append([here, beside])
        part = []
        for q, d in enumerate(delta[n]):
            if n:
                d, _ = lax.optimization_barrier((d, backs[-1][q][0]))
            ahead = leading_rows(d, ids_here[q], shift_by)
            part.append(
                {
                    o: dot_t(d, block[n, o][0]) + dot_t(ahead, block[n, o][1])
                    for o in spans
                }
            )
        backs.append(part)
        total = None
        for x, d in zip(group, (here, beside, across, diagonal)):
            term = t_dot(x, d)
            total = term if total is None else total + term
        parts = total.astype(bf16).reshape(2, len(far), rows, 2 * wide)
        got = [send(parts[:, m], leave(j, 0)) for m, j in enumerate(far)]
        got[0] = kept(parts[:, 0], got[0])
        grads.append(got)

    gated = with_layout_constraint(jnp.concatenate(gated, axis=1), Layout(major_to_minor=(0, 1)))
    out_cuts = [
        lax.dynamic_slice_in_dim(gated, (vc ^ m) * tokens, tokens, 0) for m in range(ctx)
    ]
    out_pieces = [send(out_cuts[m], leave(0, m)) for m in range(ctx)]
    out_pieces[0] = kept(out_cuts[0], out_pieces[0])
    gated_rows = placed_cols(out_pieces, c)
    layer_out = (mine.astype(f32) + gated_rows.astype(f32)).astype(bf16)

    def half_of(value, label):
        return lax.dynamic_slice_in_dim(value, label * 2 * tokens, 2 * tokens, 0)

    chip_sums = []
    for q in (0, 1):
        back = jnp.concatenate(
            [sum(backs[n][q][o] for n in range(CHUNKS)) for o in spans], axis=1
        )
        kept_rows = half_of(back, vy)
        for dy in others:
            piece = half_of(back, vy ^ dy).astype(bf16)
            kept_rows = kept_rows + send(piece, plain(0, 2 * dy)).astype(f32)
        chip_sums.append(kept_rows)
    chip_sum = in_order(*chip_sums)
    crossing = chip_sum[1].astype(bf16)
    z_got = send(crossing, plain(2, 0))

    def tokens_of(at):
        return (
            lax.dynamic_slice_in_dim(chip_sum[0], at * tokens, tokens, 0)
            + lax.dynamic_slice_in_dim(z_got, at * tokens, tokens, 0).astype(f32)
        ).astype(bf16)

    got = send(tokens_of(1 - core), plain(0, 1))
    keep = tokens_of(core)
    parts = [None] * dp
    for n, o in enumerate(spans):
        cut = slice(n * rows, (n + 1) * rows)
        parts[o], parts[o ^ 2] = keep[:, cut], got[:, cut]
    input_sum = jnp.concatenate(flipped(parts, vi), axis=1).astype(f32)
    input_grad = (cotangent[0].astype(f32) + input_sum).astype(bf16)

    totals = []
    for parts in grads:
        summed = parts[0].astype(f32)
        for part in parts[1:]:
            summed = summed + part.astype(f32)
        totals.append(summed / (length * dp))
    filter_grad = jnp.concatenate([t[:, :, :wide] for t in totals], axis=2)
    gate_grad = jnp.concatenate([t[:, :, wide:] for t in totals], axis=2)
    new_filter_w, new_filter_m, new_filter_v = adam_update(
        filter_w, filter_m, filter_v, filter_grad
    )
    new_gate_w, new_gate_m, new_gate_v = adam_update(gate_w, gate_m, gate_v, gate_grad)
    return (
        layer_out[None],
        input_grad[None],
        new_filter_w,
        new_gate_w,
        new_filter_m,
        new_filter_v,
        new_gate_m,
        new_gate_v,
    )


def solution(mesh):
    seq, par = P("dp", "ctx", None), P(None, "dp", "ctx")

    return jax.shard_map(
        per_device,
        mesh=mesh,
        in_specs=(seq, P("dp", "ctx"), P(), par, par, par, par, par, par, seq),
        out_specs=(seq, seq, par, par, par, par, par, par),
        check_vma=False,
    )
```
